512 devices in a mesh: grp: 16 (over z), dev: 32 (over x, y, core).
Axes of the slice: x: 4, y: 4, z: 16, core: 2. Of those that a mesh axis runs over, the one named last changes fastest.
Arguments:
- signs: int32 [1048576], P(('grp', 'dev')), may hold values from -1 to 1, as said below
- panel: float32 [1048576, 128], P(('grp', 'dev')), may hold values from -8 to 8
- samples: int32 [4096], replicated, may hold values from 0 to 1048575
Outputs:
- sketch: float32 [4096, 128], P(('grp', 'dev'))
The draws below stay inside these ranges and needn't reach their ends.
Inputs may be any that keep to these rules, and one draw needn't show every extreme that they name: `signs`: each entry is -1 or +1.
All inputs are finite; a program needn't handle non-finite values.
Results may differ from the reference program's by a relative error of at most 0.000086.
Values sent between devices are 32-bit elements; how exact they have to be, the bound alone decides.
No kernel may reach another device: no remote copies, remote signals or barrier semaphores. Data moves between devices by JAX's collectives and lax.ppermute only.
A program may use at most 64 MiB of HBM per device.

```python
import jax
import jax.numpy as jnp

PANEL = 128
ROWS = 1048576
SAMPLES = 4096


def draw_signs(key, part):
    flips = jax.random.randint(key, (ROWS,), 0, 2, dtype=jnp.int32)
    return 2 * flips - 1


def touch_ends(entries, rng, smallest, top_value):
    longest = entries.shape.index(max(entries.shape))
    spots = []
    for shift in (0, 1):
        where = [jax.random.randint(jax.random.fold_in(rng, axis), (), 0, length) for axis, length in enumerate(entries.shape)]
        where[longest] = (where[longest] + shift) % entries.shape[longest]
        spots.append(tuple(where))
    return entries.at[spots[0]].set(smallest).at[spots[1]].set(top_value)


def levels(own_key, shape, cuts, smallest, top_value):
    factor_of = 1.0
    for axis_at, shards_of in cuts:
        steps = jax.random.uniform(jax.random.fold_in(jax.random.fold_in(own_key, 6), axis_at), (shards_of,), jnp.float32, smallest / len(cuts), top_value / len(cuts))
        factor_of = factor_of * jnp.repeat(jnp.exp(steps), shape[axis_at] // shards_of).reshape((-1,) + (1,) * (len(shape) - 1 - axis_at))
    return factor_of


def gaussian(rng, extent, scale, limit, cuts=(), kind=jnp.bfloat16):
    values = jax.random.normal(rng, extent, jnp.float32) * scale
    if len(cuts) > 0:
        values = levels(rng, extent, cuts, -0.22, 0.18) * values
    return jnp.clip(values, min=-limit, max=limit).astype(kind)


def setup_inputs(seed: int = 0) -> dict:
    seeds = jax.random.split(jax.random.key(seed), 4)
    signs = draw_signs(jax.random.fold_in(seeds[3], 71), 0)
    panel = gaussian(seeds[1], (ROWS, PANEL), 1.0, 8.0, ((0, 512),), jnp.float32)
    samples = touch_ends(jax.random.randint(seeds[2], (SAMPLES,), 0, ROWS), jax.random.fold_in(seeds[2], 1), 0, ROWS - 1).astype(jnp.int32)
    return {"signs": signs, "panel": panel, "samples": samples}


def reference(signs, panel, samples):
    flipped = panel * signs.astype(panel.dtype)[:, None]
    total = flipped.shape[0]
    width = flipped.shape[1]
    mixed = flipped
    half = 1
    for level in range(total.bit_length() - 1):
        pairs = mixed.reshape(total // (2 * half), 2, half, width)
        first = pairs[:, 0]
        second = pairs[:, 1]
        mixed = jnp.stack([first + second, first - second], axis=1).reshape(total, width)
        half = half * 2
    mixed = mixed / jnp.sqrt(jnp.asarray(total, mixed.dtype))
    return jnp.take(mixed, samples, axis=0)
```

```python
import functools
import math

import jax
import jax.numpy as jnp
from jax import lax
from jax.experimental import pallas as pl
from jax.experimental.pallas import tpu as pltpu
from jax.sharding import PartitionSpec as P

LANES = 128
SUB = 8


def odd_parity(value, bits):
    shift = 1
    while shift < bits:
        shift *= 2
    while shift > 1:
        shift //= 2
        value = value ^ (value >> shift)
    return value & 1


def columns_of(row):
    return jnp.broadcast_to(row, (LANES, LANES)).T


def partial_kernel(where_ref, samples_ref, signs_ref, panel_ref, out_ref, split_ref, *, tile):
    me, core = where_ref[0], where_ref[1]
    rows = panel_ref.shape[0]
    blocks = rows // LANES
    low = rows.bit_length() - 1
    lane_bits = LANES.bit_length() - 1

    for block in range(blocks):
        span = pl.ds(block * LANES, LANES)
        flipped = panel_ref[span, :] * columns_of(signs_ref[block : block + 1, :].astype(jnp.float32))
        high = flipped.astype(jnp.bfloat16)
        split_ref[span, :LANES] = high
        split_ref[span, LANES:] = (flipped - high.astype(jnp.float32)).astype(jnp.bfloat16)

    picks = samples_ref[...]
    device_odd = odd_parity((picks >> low) & me, 16)
    picks = (picks & (LANES - 1)) | (device_odd << lane_bits) | (((picks & (rows - 1)) >> lane_bits) << (lane_bits + 1))
    lane = lax.broadcasted_iota(jnp.int32, (tile * LANES // 2, LANES), 1) | LANES
    weights = split_ref[...]
    one, minus = jnp.float32(1), jnp.float32(-1)
    per_group = out_ref.shape[0] * SUB * 2 // LANES

    for start in range(0, picks.shape[0], tile):
        parts = []
        for line in range(start, start + tile):
            pairs = columns_of(picks[line : line + 1, :]).reshape(LANES // (2 * SUB), 2, SUB, LANES)
            parts.append(jnp.where(core == 0, pairs[:, 0], pairs[:, 1]).reshape(LANES // 2, LANES))
        own = jnp.concatenate(parts, axis=0)
        table = [jnp.where(odd_parity(own & lane, lane_bits + 1) == 0, one, minus).astype(jnp.bfloat16)]
        for level in range(blocks.bit_length() - 1):
            turn = jnp.where(own & (2 * LANES << level) == 0, one, minus).astype(jnp.bfloat16)
            table = table + [entry * turn for entry in table]
        left = jnp.concatenate(table, axis=1)
        both = jnp.dot(left, weights, preferred_element_type=jnp.float32)
        total = both[:, :LANES] + both[:, LANES:]
        groups = tile // per_group
        total = total.reshape(groups, out_ref.shape[0], SUB, LANES)
        for group in range(groups):
            out_ref[:, start // per_group + group] = total[group]


def partial_rows(where, samples, signs, panel, n_chip, n_grp):
    rows = panel.shape[0]
    vmem = pl.BlockSpec(memory_space=pltpu.VMEM)
    return pl.pallas_call(
        functools.partial(partial_kernel, tile=8),
        out_shape=jax.ShapeDtypeStruct((n_chip, n_grp, SUB, LANES), jnp.float32),
        in_specs=[pl.BlockSpec(memory_space=pltpu.SMEM), vmem, vmem, vmem],
        out_specs=vmem,
        scratch_shapes=[pltpu.VMEM((rows, 2 * LANES), jnp.bfloat16)],
        cost_estimate=pl.CostEstimate(flops=2 * 2048 * 2048 * 256, bytes_accessed=3 << 20, transcendentals=0),
    )(where, samples, signs, panel)


def local(signs, panel, samples):
    rows, width = panel.shape
    n_dev = lax.axis_size("dev")
    n_grp = lax.axis_size("grp")
    n_chip = n_dev // 2
    member = lax.axis_index("dev")
    core = member & 1
    me = lax.axis_index("grp") * n_dev + member
    scale = 1.0 / math.sqrt(rows * n_dev * n_grp)
    samples = samples.reshape(-1, LANES)
    signs = signs.reshape(-1, LANES)

    def part(side):
        return partial_rows(jnp.stack([me, side]), samples, signs, panel, n_chip, n_grp)

    swap = [(source, source ^ 1) for source in range(n_dev)]
    theirs = lax.ppermute(part(1 - core), "dev", swap)
    chip = part(core) + theirs
    cores = [[chip_at * 2 + side for chip_at in range(n_chip)] for side in range(2)]
    plane = lax.all_to_all(
        chip.reshape(n_chip, n_grp * SUB, width), "dev", 0, 0, axis_index_groups=cores, tiled=True
    ).sum(axis=0)
    column = lax.all_to_all(plane.reshape(n_grp, SUB, width), "grp", 0, 0, tiled=True)
    return column.sum(axis=0) * scale


def solution(mesh):
    return jax.shard_map(
        local,
        mesh=mesh,
        in_specs=(P(("grp", "dev")), P(("grp", "dev"), None), P()),
        out_specs=P(("grp", "dev"), None),
        check_vma=False,
    )
```

```python
import functools
import math

import jax
import jax.numpy as jnp
from jax import lax
from jax.experimental import pallas as pl
from jax.experimental.pallas import tpu as pltpu
from jax.sharding import PartitionSpec as P

LANES = 128
SUB = 8
LANE_BITS = LANES.bit_length() - 1
TILE = 8
CHUNKS = 4


def odd_parity(value, bits):
    shift = 1
    while shift < bits:
        shift *= 2
    while shift > 1:
        shift //= 2
        value = value ^ (value >> shift)
    return value & 1


def columns_of(row):
    return jnp.broadcast_to(row, (LANES, LANES)).T


def coded(samples, rows, me):
    low = rows.bit_length() - 1
    device_odd = odd_parity((samples >> low) & me, 16)
    return (samples & (LANES - 1)) | (device_odd << LANE_BITS) | ((samples & (rows - LANES)) << 1)


def sign_rows(codes, start, blocks, side):
    parts = []
    for line in range(start, start + TILE):
        pairs = columns_of(codes[line : line + 1, :]).reshape(LANES // (2 * SUB), 2, SUB, LANES)
        parts.append(jnp.where(side == 0, pairs[:, 0], pairs[:, 1]).reshape(LANES // 2, LANES))
    own = jnp.concatenate(parts, axis=0)
    lane = lax.broadcasted_iota(jnp.int32, own.shape, 1) | LANES
    one, minus = jnp.float32(1), jnp.float32(-1)
    table = [jnp.where(odd_parity(own & lane, LANE_BITS + 1) == 0, one, minus).astype(jnp.bfloat16)]
    for level in range(blocks.bit_length() - 1):
        turn = jnp.where(own & (2 * LANES << level) == 0, one, minus).astype(jnp.bfloat16)
        table = table + [entry * turn for entry in table]
    return table


def sum_samples(codes, side, split_ref, out_ref, table=None):
    lines = codes.shape[0]
    blocks = split_ref.shape[0] // LANES
    chips = out_ref.shape[0]
    per_group = chips * SUB * 2 // LANES
    groups = TILE // per_group
    weights = split_ref[...]
    for start in range(0, lines, TILE):
        if start or table is None:
            table = sign_rows(codes, start, blocks, side)
        both = jnp.dot(jnp.concatenate(table, axis=1), weights, preferred_element_type=jnp.float32)
        total = (both[:, :LANES] + both[:, LANES:]).reshape(groups, chips, SUB, LANES)
        for group in range(groups):
            out_ref[:, start // per_group + group] = total[group]


def position():
    member = lax.axis_index("dev")
    return lax.axis_index("grp") * lax.axis_size("dev") + member, member & 1


def first_kernel(samples_ref, signs_ref, panel_ref, out_ref, split_ref, codes_ref, picks_ref, flips_ref, rows_ref, sems):
    me, core = position()
    rows = rows_ref.shape[0]
    blocks = rows // LANES
    part = rows // CHUNKS
    small = [
        pltpu.make_async_copy(samples_ref, picks_ref, sems.at[CHUNKS]),
        pltpu.make_async_copy(signs_ref, flips_ref, sems.at[CHUNKS + 1]),
    ]
    copies = []
    for chunk in range(CHUNKS):
        span = pl.ds(chunk * part, part)
        copies.append(pltpu.make_async_copy(panel_ref.at[span], rows_ref.at[span], sems.at[chunk]))
    for copy in small + copies:
        copy.start()
    small[0].wait()
    codes = coded(picks_ref[...], rows, me)
    codes_ref[...] = codes
    table = sign_rows(codes, 0, blocks, 1 - core)
    small[1].wait()
    for block in range(blocks):
        if block % (blocks // CHUNKS) == 0:
            copies[block // (blocks // CHUNKS)].wait()
        span = pl.ds(block * LANES, LANES)
        flipped = rows_ref[span, :] * columns_of(flips_ref[block : block + 1, :].astype(jnp.float32))
        high = flipped.astype(jnp.bfloat16)
        split_ref[span, :LANES] = high
        split_ref[span, LANES:] = (flipped - high.astype(jnp.float32)).astype(jnp.bfloat16)
    sum_samples(codes, 1 - core, split_ref, out_ref, table)


def second_kernel(codes_ref, split_ref, out_ref):
    core = lax.axis_index("dev") & 1
    sum_samples(codes_ref[...], core, split_ref, out_ref)


def local(signs, panel, samples):
    rows, width = panel.shape
    n_dev = lax.axis_size("dev")
    n_grp = lax.axis_size("grp")
    n_chip = n_dev // 2
    scale = 1.0 / math.sqrt(rows * n_dev * n_grp)
    samples = samples.reshape(-1, LANES)
    signs = signs.reshape(-1, LANES)
    vmem = pl.BlockSpec(memory_space=pltpu.VMEM)
    hbm = pl.BlockSpec(memory_space=pltpu.HBM)
    partial = pltpu.VMEM((n_chip, n_grp, SUB, LANES), jnp.float32)
    params = pltpu.CompilerParams(vmem_limit_bytes=16 << 20)
    cost = pl.CostEstimate(flops=2 * 2048 * 2048 * 256, bytes_accessed=3 << 20, transcendentals=0)

    theirs, split, codes = pl.pallas_call(
        first_kernel,
        out_shape=(partial, pltpu.VMEM((rows, 2 * LANES), jnp.bfloat16), pltpu.VMEM(samples.shape, jnp.int32)),
        in_specs=[hbm, hbm, hbm],
        out_specs=(vmem, vmem, vmem),
        scratch_shapes=[
            pltpu.VMEM(samples.shape, jnp.int32),
            pltpu.VMEM(signs.shape, jnp.int32),
            pltpu.VMEM((rows, LANES), jnp.float32),
            pltpu.SemaphoreType.DMA((CHUNKS + 2,)),
        ],
        compiler_params=params,
        cost_estimate=cost,
    )(*(pltpu.with_memory_space_constraint(value, pltpu.HBM) for value in (samples, signs, panel)))
    theirs = lax.ppermute(theirs, "dev", [(source, source ^ 1) for source in range(n_dev)])
    ours = pl.pallas_call(
        second_kernel,
        out_shape=partial,
        in_specs=[vmem, vmem],
        out_specs=vmem,
        compiler_params=params,
        cost_estimate=cost,
    )(codes, split)
    chip = ours + theirs
    cores = [[chip_at * 2 + side for chip_at in range(n_chip)] for side in range(2)]
    plane = lax.all_to_all(
        chip.reshape(n_chip, n_grp * SUB, width), "dev", 0, 0, axis_index_groups=cores, tiled=True
    ).sum(axis=0)
    column = lax.all_to_all(plane.reshape(n_grp, SUB, width), "grp", 0, 0, tiled=True)
    return column.sum(axis=0) * scale


def solution(mesh):
    return jax.shard_map(
        local,
        mesh=mesh,
        in_specs=(P(("grp", "dev")), P(("grp", "dev"), None), P()),
        out_specs=P(("grp", "dev"), None),
        check_vma=False,
    )
```

```python
import functools
import math

import jax
import jax.numpy as jnp
from jax import lax
from jax.experimental import pallas as pl
from jax.experimental.pallas import tpu as pltpu
from jax.sharding import PartitionSpec as P

LANES = 128
SUB = 8
LANE_BITS = LANES.bit_length() - 1
TILE = 8
CHUNKS = 4
FIRST_GROUP = 8
FIRST_CHIP = 15


def odd_parity(value, bits):
    shift = 1
    while shift < bits:
        shift *= 2
    while shift > 1:
        shift //= 2
        value = value ^ (value >> shift)
    return value & 1


def columns_of(row):
    return jnp.broadcast_to(row, (LANES, LANES)).T


def coded(samples, rows, me):
    low = rows.bit_length() - 1
    device_odd = odd_parity((samples >> low) & me, 16)
    return (samples & (LANES - 1)) | (device_odd << LANE_BITS) | ((samples & (rows - LANES)) << 1)


def sign_rows(codes, start, blocks, side):
    parts = []
    for line in range(start, start + TILE):
        pairs = columns_of(codes[line : line + 1, :]).reshape(LANES // (2 * SUB), 2, SUB, LANES)
        parts.append(jnp.where(side == 0, pairs[:, 0], pairs[:, 1]).reshape(LANES // 2, LANES))
    own = jnp.concatenate(parts, axis=0)
    lane = lax.broadcasted_iota(jnp.int32, own.shape, 1) | LANES
    one, minus = jnp.float32(1), jnp.float32(-1)
    table = [jnp.where(odd_parity(own & lane, LANE_BITS + 1) == 0, one, minus).astype(jnp.bfloat16)]
    for level in range(blocks.bit_length() - 1):
        turn = jnp.where(own & (2 * LANES << level) == 0, one, minus).astype(jnp.bfloat16)
        table = table + [entry * turn for entry in table]
    return table


def sum_samples(codes, side, split_ref, out_ref, table=None):
    lines = codes.shape[0]
    blocks = split_ref.shape[0] // LANES
    chips = out_ref.shape[0]
    per_group = chips * SUB * 2 // LANES
    groups = TILE // per_group
    weights = split_ref[...]
    for start in range(0, lines, TILE):
        if start or table is None:
            table = sign_rows(codes, start, blocks, side)
        both = jnp.dot(jnp.concatenate(table, axis=1), weights, preferred_element_type=jnp.float32)
        total = (both[:, :LANES] + both[:, LANES:]).reshape(groups, chips, SUB, LANES)
        for group in range(groups):
            place = (start // per_group + group - FIRST_GROUP) % out_ref.shape[1]
            for chip in range(chips):
                out_ref[(chip - FIRST_CHIP) % chips, place] = total[group, chip]


def position():
    member = lax.axis_index("dev")
    return lax.axis_index("grp") * lax.axis_size("dev") + member, member & 1


def first_kernel(samples_ref, signs_ref, panel_ref, out_ref, split_ref, codes_ref, picks_ref, flips_ref, rows_ref, sems):
    me, core = position()
    rows = rows_ref.shape[0]
    blocks = rows // LANES
    part = rows // CHUNKS
    small = [
        pltpu.make_async_copy(samples_ref, picks_ref, sems.at[CHUNKS]),
        pltpu.make_async_copy(signs_ref, flips_ref, sems.at[CHUNKS + 1]),
    ]
    copies = []
    for chunk in range(CHUNKS):
        span = pl.ds(chunk * part, part)
        copies.append(pltpu.make_async_copy(panel_ref.at[span], rows_ref.at[span], sems.at[chunk]))
    for copy in small + copies:
        copy.start()
    small[0].wait()
    codes = coded(picks_ref[...], rows, me)
    codes_ref[...] = codes
    table = sign_rows(codes, 0, blocks, 1 - core)
    small[1].wait()
    for block in range(blocks):
        if block % (blocks // CHUNKS) == 0:
            copies[block // (blocks // CHUNKS)].wait()
        span = pl.ds(block * LANES, LANES)
        flipped = rows_ref[span, :] * columns_of(flips_ref[block : block + 1, :].astype(jnp.float32))
        high = flipped.astype(jnp.bfloat16)
        split_ref[span, :LANES] = high
        split_ref[span, LANES:] = (flipped - high.astype(jnp.float32)).astype(jnp.bfloat16)
    sum_samples(codes, 1 - core, split_ref, out_ref, table)


def second_kernel(codes_ref, split_ref, out_ref):
    core = lax.axis_index("dev") & 1
    sum_samples(codes_ref[...], core, split_ref, out_ref)


def local(signs, panel, samples):
    rows, width = panel.shape
    n_dev = lax.axis_size("dev")
    n_grp = lax.axis_size("grp")
    n_chip = n_dev // 2
    scale = 1.0 / math.sqrt(rows * n_dev * n_grp)
    samples = samples.reshape(-1, LANES)
    signs = signs.reshape(-1, LANES)
    vmem = pl.BlockSpec(memory_space=pltpu.VMEM)
    hbm = pl.BlockSpec(memory_space=pltpu.HBM)
    partial = pltpu.VMEM((n_chip, n_grp, SUB, LANES), jnp.float32)
    params = pltpu.CompilerParams(vmem_limit_bytes=16 << 20)
    cost = pl.CostEstimate(flops=2 * 2048 * 2048 * 256, bytes_accessed=3 << 20, transcendentals=0)

    theirs, split, codes = pl.pallas_call(
        first_kernel,
        out_shape=(partial, pltpu.VMEM((rows, 2 * LANES), jnp.bfloat16), pltpu.VMEM(samples.shape, jnp.int32)),
        in_specs=[hbm, hbm, hbm],
        out_specs=(vmem, vmem, vmem),
        scratch_shapes=[
            pltpu.VMEM(samples.shape, jnp.int32),
            pltpu.VMEM(signs.shape, jnp.int32),
            pltpu.VMEM((rows, LANES), jnp.float32),
            pltpu.SemaphoreType.DMA((CHUNKS + 2,)),
        ],
        compiler_params=params,
        cost_estimate=cost,
    )(*(pltpu.with_memory_space_constraint(value, pltpu.HBM) for value in (samples, signs, panel)))
    theirs = lax.ppermute(theirs, "dev", [(source, source ^ 1) for source in range(n_dev)])
    ours = pl.pallas_call(
        second_kernel,
        out_shape=partial,
        in_specs=[vmem, vmem],
        out_specs=vmem,
        compiler_params=params,
        cost_estimate=cost,
    )(codes, split)
    chip = ours + theirs
    chips = [(chip_at + FIRST_CHIP) % n_chip for chip_at in range(n_chip)]
    plane = lax.all_to_all(
        chip.reshape(n_chip, n_grp * SUB, width),
        "dev",
        0,
        0,
        axis_index_groups=[[chip_at * 2 + side for chip_at in chips] for side in range(2)],
        tiled=True,
    ).sum(axis=0)
    column = lax.all_to_all(
        plane.reshape(n_grp, SUB, width),
        "grp",
        0,
        0,
        axis_index_groups=[[(group + FIRST_GROUP) % n_grp for group in range(n_grp)]],
        tiled=True,
    )
    return column.sum(axis=0) * scale


def solution(mesh):
    return jax.shard_map(
        local,
        mesh=mesh,
        in_specs=(P(("grp", "dev")), P(("grp", "dev"), None), P()),
        out_specs=P(("grp", "dev"), None),
        check_vma=False,
    )
```

```python
import functools
import math

import jax
import jax.numpy as jnp
from jax import lax
from jax.experimental import pallas as pl
from jax.experimental.pallas import tpu as pltpu
from jax.sharding import PartitionSpec as P

LANES = 128
SUB = 8
LANE_BITS = LANES.bit_length() - 1
TILE = 8
CHUNKS = 4
GROUPS = tuple((8 + at) % 16 for at in range(16))
CHIPS = tuple((10 + at) % 16 for at in range(16))


def odd_parity(value):
    return lax.population_count(value) & 1


def columns_of(row):
    return jnp.broadcast_to(row, (LANES, LANES)).T


def coded(samples, rows, me):
    low = rows.bit_length() - 1
    device_odd = odd_parity((samples >> low) & me)
    return (samples & (LANES - 1)) | (device_odd << LANE_BITS) | ((samples & (rows - LANES)) << 1)


def sign_rows(codes, start, blocks, side):
    parts = []
    for line in range(start, start + TILE):
        pairs = columns_of(codes[line : line + 1, :]).reshape(LANES // (2 * SUB), 2, SUB, LANES)
        parts.append(jnp.where(side == 0, pairs[:, 0], pairs[:, 1]).reshape(LANES // 2, LANES))
    own = jnp.concatenate(parts, axis=0)
    lane = lax.broadcasted_iota(jnp.int32, own.shape, 1) | LANES
    one, minus = jnp.float32(1), jnp.float32(-1)
    table = [jnp.where(odd_parity(own & lane) == 0, one, minus).astype(jnp.bfloat16)]
    for level in range(blocks.bit_length() - 1):
        turn = jnp.where(own & (2 * LANES << level) == 0, one, minus).astype(jnp.bfloat16)
        table = table + [entry * turn for entry in table]
    return table


def sum_samples(codes, side, split_ref, out_ref, table=None):
    lines = codes.shape[0]
    blocks = split_ref.shape[0] // LANES
    chips = out_ref.shape[0]
    per_group = chips * SUB * 2 // LANES
    groups = TILE // per_group
    weights = split_ref[...]
    for start in range(0, lines, TILE):
        if start or table is None:
            table = sign_rows(codes, start, blocks, side)
        both = jnp.dot(jnp.concatenate(table, axis=1), weights, preferred_element_type=jnp.float32)
        total = (both[:, :LANES] + both[:, LANES:]).reshape(groups, chips, SUB, LANES)
        for group in range(groups):
            place = GROUPS.index(start // per_group + group)
            for chip in range(chips):
                out_ref[CHIPS.index(chip), place] = total[group, chip]


def position():
    member = lax.axis_index("dev")
    return lax.axis_index("grp") * lax.axis_size("dev") + member, member & 1


def first_kernel(samples_ref, signs_ref, panel_ref, out_ref, split_ref, codes_ref, picks_ref, flips_ref, rows_ref, sems):
    me, core = position()
    rows = rows_ref.shape[0]
    blocks = rows // LANES
    part = rows // CHUNKS
    small = [
        pltpu.make_async_copy(samples_ref, picks_ref, sems.at[CHUNKS]),
        pltpu.make_async_copy(signs_ref, flips_ref, sems.at[CHUNKS + 1]),
    ]
    copies = []
    for chunk in range(CHUNKS):
        span = pl.ds(chunk * part, part)
        copies.append(pltpu.make_async_copy(panel_ref.at[span], rows_ref.at[span], sems.at[chunk]))
    for copy in small + copies:
        copy.start()
    small[0].wait()
    codes = coded(picks_ref[...], rows, me)
    codes_ref[...] = codes
    table = sign_rows(codes, 0, blocks, 1 - core)
    for copy in small[1:] + copies:
        copy.wait()
    for block in range(blocks):
        span = pl.ds(block * LANES, LANES)
        flipped = rows_ref[span, :] * columns_of(flips_ref[block : block + 1, :].astype(jnp.float32))
        high = flipped.astype(jnp.bfloat16)
        split_ref[span, :LANES] = high
        split_ref[span, LANES:] = (flipped - high.astype(jnp.float32)).astype(jnp.bfloat16)
    sum_samples(codes, 1 - core, split_ref, out_ref, table)


def second_kernel(codes_ref, split_ref, out_ref):
    core = lax.axis_index("dev") & 1
    sum_samples(codes_ref[...], core, split_ref, out_ref)


def local(signs, panel, samples):
    rows, width = panel.shape
    n_dev = lax.axis_size("dev")
    n_grp = lax.axis_size("grp")
    n_chip = n_dev // 2
    scale = 1.0 / math.sqrt(rows * n_dev * n_grp)
    samples = samples.reshape(-1, LANES)
    signs = signs.reshape(-1, LANES)
    vmem = pl.BlockSpec(memory_space=pltpu.VMEM)
    hbm = pl.BlockSpec(memory_space=pltpu.HBM)
    partial = pltpu.VMEM((n_chip, n_grp, SUB, LANES), jnp.float32)
    params = pltpu.CompilerParams(vmem_limit_bytes=16 << 20)
    cost = pl.CostEstimate(flops=2 * 2048 * 2048 * 256, bytes_accessed=3 << 20, transcendentals=0)

    theirs, split, codes = pl.pallas_call(
        first_kernel,
        out_shape=(partial, pltpu.VMEM((rows, 2 * LANES), jnp.bfloat16), pltpu.VMEM(samples.shape, jnp.int32)),
        in_specs=[hbm, hbm, hbm],
        out_specs=(vmem, vmem, vmem),
        scratch_shapes=[
            pltpu.VMEM(samples.shape, jnp.int32),
            pltpu.VMEM(signs.shape, jnp.int32),
            pltpu.VMEM((rows, LANES), jnp.float32),
            pltpu.SemaphoreType.DMA((CHUNKS + 2,)),
        ],
        compiler_params=params,
        cost_estimate=cost,
    )(*(pltpu.with_memory_space_constraint(value, pltpu.HBM) for value in (samples, signs, panel)))
    theirs = lax.ppermute(theirs, "dev", [(source, source ^ 1) for source in range(n_dev)])
    ours = pl.pallas_call(
        second_kernel,
        out_shape=partial,
        in_specs=[vmem, vmem],
        out_specs=vmem,
        compiler_params=params,
        cost_estimate=cost,
    )(codes, split)
    chip = ours + theirs
    plane = lax.all_to_all(
        chip.reshape(n_chip, n_grp * SUB, width),
        "dev",
        0,
        0,
        axis_index_groups=[[chip_at * 2 + side for chip_at in CHIPS] for side in range(2)],
        tiled=True,
    ).sum(axis=0)
    column = lax.all_to_all(
        plane.reshape(n_grp, SUB, width),
        "grp",
        0,
        0,
        axis_index_groups=[GROUPS],
        tiled=True,
    )
    return column.sum(axis=0) * scale


def solution(mesh):
    return jax.shard_map(
        local,
        mesh=mesh,
        in_specs=(P(("grp", "dev")), P(("grp", "dev"), None), P()),
        out_specs=P(("grp", "dev"), None),
        check_vma=False,
    )
```

```python
import functools
import math

import jax
import jax.numpy as jnp
from jax import lax
from jax.experimental import pallas as pl
from jax.experimental.pallas import tpu as pltpu
from jax.sharding import PartitionSpec as P

LANES = 128
SUB = 8
LANE_BITS = LANES.bit_length() - 1
TILE = 4
CHUNKS = 4
GROUPS = (9, 0, 15, 1, 14, 2, 13, 3, 12, 4, 11, 5, 10, 6, 8, 7)
CHIPS = tuple((10 + at) % 16 for at in range(16))


def odd_parity(value):
    return lax.population_count(value) & 1


def columns_of(row):
    return jnp.broadcast_to(row, (LANES, LANES)).T


def coded(samples, rows, me):
    low = rows.bit_length() - 1
    device_odd = odd_parity((samples >> low) & me)
    return (samples & (LANES - 1)) | (device_odd << LANE_BITS) | ((samples & (rows - LANES)) << 1)


def sign_rows(codes, start, blocks, side):
    parts = []
    for line in range(start, start + TILE):
        pairs = columns_of(codes[line : line + 1, :]).reshape(LANES // (2 * SUB), 2, SUB, LANES)
        parts.append(jnp.where(side == 0, pairs[:, 0], pairs[:, 1]).reshape(LANES // 2, LANES))
    own = jnp.concatenate(parts, axis=0)
    lane = lax.broadcasted_iota(jnp.int32, own.shape, 1) | LANES
    one, minus = jnp.float32(1), jnp.float32(-1)
    table = [jnp.where(odd_parity(own & lane) == 0, one, minus).astype(jnp.bfloat16)]
    for level in range(blocks.bit_length() - 1):
        turn = jnp.where(own & (2 * LANES << level) == 0, one, minus).astype(jnp.bfloat16)
        table = table + [entry * turn for entry in table]
    return table


def sum_samples(codes, side, split_ref, out_ref, table=None):
    lines = codes.shape[0]
    blocks = split_ref.shape[0] // LANES
    chips = out_ref.shape[0]
    per_group = chips * SUB * 2 // LANES
    groups = TILE // per_group
    weights = split_ref[...]
    for start in range(0, lines, TILE):
        if start or table is None:
            table = sign_rows(codes, start, blocks, side)
        both = jnp.dot(jnp.concatenate(table, axis=1), weights, preferred_element_type=jnp.float32)
        total = (both[:, :LANES] + both[:, LANES:]).reshape(groups, chips, SUB, LANES)
        for group in range(groups):
            place = GROUPS.index(start // per_group + group)
            for chip in range(chips):
                out_ref[CHIPS.index(chip), place] = total[group, chip]


def position():
    member = lax.axis_index("dev")
    return lax.axis_index("grp") * lax.axis_size("dev") + member, member & 1


def first_kernel(samples_ref, signs_ref, panel_ref, out_ref, split_ref, codes_ref, picks_ref, flips_ref, rows_ref, sems):
    me, core = position()
    rows = rows_ref.shape[0]
    blocks = rows // LANES
    part = rows // CHUNKS
    small = [
        pltpu.make_async_copy(samples_ref, picks_ref, sems.at[CHUNKS]),
        pltpu.make_async_copy(signs_ref, flips_ref, sems.at[CHUNKS + 1]),
    ]
    copies = []
    for chunk in range(CHUNKS):
        span = pl.ds(chunk * part, part)
        copies.append(pltpu.make_async_copy(panel_ref.at[span], rows_ref.at[span], sems.at[chunk]))
    for chunk, copy in enumerate(copies):
        copy.start(priority=chunk % 2)
    for copy in small:
        copy.start()
    small[0].wait()
    codes = coded(picks_ref[...], rows, me)
    codes_ref[...] = codes
    table = sign_rows(codes, 0, blocks, 1 - core)
    for copy in small[1:] + copies:
        copy.wait()
    for block in range(blocks):
        span = pl.ds(block * LANES, LANES)
        flipped = rows_ref[span, :] * columns_of(flips_ref[block : block + 1, :].astype(jnp.float32))
        high = flipped.astype(jnp.bfloat16)
        split_ref[span, :LANES] = high
        split_ref[span, LANES:] = (flipped - high.astype(jnp.float32)).astype(jnp.bfloat16)
    sum_samples(codes, 1 - core, split_ref, out_ref, table)


def second_kernel(codes_ref, split_ref, out_ref):
    core = lax.axis_index("dev") & 1
    sum_samples(codes_ref[...], core, split_ref, out_ref)


def local(signs, panel, samples):
    rows, width = panel.shape
    n_dev = lax.axis_size("dev")
    n_grp = lax.axis_size("grp")
    n_chip = n_dev // 2
    scale = 1.0 / math.sqrt(rows * n_dev * n_grp)
    samples = samples.reshape(-1, LANES)
    signs = signs.reshape(-1, LANES)
    vmem = pl.BlockSpec(memory_space=pltpu.VMEM)
    hbm = pl.BlockSpec(memory_space=pltpu.HBM)
    partial = pltpu.VMEM((n_chip, n_grp, SUB, LANES), jnp.float32)
    params = pltpu.CompilerParams(vmem_limit_bytes=16 << 20)
    cost = pl.CostEstimate(flops=2 * 2048 * 2048 * 256, bytes_accessed=3 << 20, transcendentals=0)

    theirs, split, codes = pl.pallas_call(
        first_kernel,
        out_shape=(partial, pltpu.VMEM((rows, 2 * LANES), jnp.bfloat16), pltpu.VMEM(samples.shape, jnp.int32)),
        in_specs=[hbm, hbm, hbm],
        out_specs=(vmem, vmem, vmem),
        scratch_shapes=[
            pltpu.VMEM(samples.shape, jnp.int32),
            pltpu.VMEM(signs.shape, jnp.int32),
            pltpu.VMEM((rows, LANES), jnp.float32),
            pltpu.SemaphoreType.DMA((CHUNKS + 2,)),
        ],
        compiler_params=params,
        cost_estimate=cost,
    )(*(pltpu.with_memory_space_constraint(value, pltpu.HBM) for value in (samples, signs, panel)))
    theirs = lax.ppermute(theirs, "dev", [(source, source ^ 1) for source in range(n_dev)])
    ours = pl.pallas_call(
        second_kernel,
        out_shape=partial,
        in_specs=[vmem, vmem],
        out_specs=vmem,
        compiler_params=params,
        cost_estimate=cost,
    )(codes, split)
    chip = ours + theirs
    plane = lax.all_to_all(
        chip.reshape(n_chip, n_grp * SUB, width),
        "dev",
        0,
        0,
        axis_index_groups=[[chip_at * 2 + side for chip_at in CHIPS] for side in range(2)],
        tiled=True,
    ).sum(axis=0)
    column = lax.all_to_all(
        plane.reshape(n_grp, SUB, width),
        "grp",
        0,
        0,
        axis_index_groups=[GROUPS],
        tiled=True,
    )
    return column.sum(axis=0) * scale


def solution(mesh):
    return jax.shard_map(
        local,
        mesh=mesh,
        in_specs=(P(("grp", "dev")), P(("grp", "dev"), None), P()),
        out_specs=P(("grp", "dev"), None),
        check_vma=False,
    )
```

```python
import functools
import math

import jax
import jax.numpy as jnp
from jax import lax
from jax.experimental import pallas as pl
from jax.experimental.pallas import tpu as pltpu
from jax.sharding import PartitionSpec as P

LANES = 128
SUB = 8
LANE_BITS = LANES.bit_length() - 1
TILE = 4
CHUNKS = 4
GROUPS = (9, 0, 15, 1, 14, 2, 13, 3, 12, 4, 11, 5, 10, 6, 8, 7)
CHIPS = tuple((10 + at) % 16 for at in range(16))


def odd_parity(value):
    return lax.population_count(value) & 1


def columns_of(row):
    return jnp.broadcast_to(row, (LANES, LANES)).T


def coded(samples, rows, me):
    low = rows.bit_length() - 1
    device_odd = odd_parity((samples >> low) & me)
    return (samples & (LANES - 1)) | (device_odd << LANE_BITS) | ((samples & (rows - LANES)) << 1)


def sign_rows(codes, start, blocks, side):
    parts = []
    for line in range(start, start + TILE):
        pairs = columns_of(codes[line : line + 1, :]).reshape(LANES // (2 * SUB), 2, SUB, LANES)
        parts.append(jnp.where(side == 0, pairs[:, 0], pairs[:, 1]).reshape(LANES // 2, LANES))
    own = jnp.concatenate(parts, axis=0)
    lane = lax.broadcasted_iota(jnp.int32, own.shape, 1) | LANES
    one, minus = jnp.float32(1), jnp.float32(-1)
    table = [jnp.where(odd_parity(own & lane) == 0, one, minus).astype(jnp.bfloat16)]
    for level in range(blocks.bit_length() - 1):
        turn = jnp.where(own & (2 * LANES << level) == 0, one, minus).astype(jnp.bfloat16)
        table = table + [entry * turn for entry in table]
    return table


def sum_samples(codes, side, split_ref, out_ref, table=None):
    lines = codes.shape[0]
    blocks = split_ref.shape[0] // LANES
    chips = out_ref.shape[0]
    per_group = chips * SUB * 2 // LANES
    groups = TILE // per_group
    weights = split_ref[...]
    for start in range(0, lines, TILE):
        if start or table is None:
            table = sign_rows(codes, start, blocks, side)
        both = jnp.dot(jnp.concatenate(table, axis=1), weights, preferred_element_type=jnp.float32)
        total = (both[:, :LANES] + both[:, LANES:]).reshape(groups, chips, SUB, LANES)
        for group in range(groups):
            place = GROUPS.index(start // per_group + group)
            for chip in range(chips):
                out_ref[CHIPS.index(chip), place] = total[group, chip]


def position():
    member = lax.axis_index("dev")
    return lax.axis_index("grp") * lax.axis_size("dev") + member, member & 1


def first_kernel(samples_ref, signs_ref, panel_ref, out_ref, split_ref, codes_ref, picks_ref, flips_ref, rows_ref, sems):
    me, core = position()
    rows = rows_ref.shape[0]
    blocks = rows // LANES
    part = rows // CHUNKS
    small = [
        pltpu.make_async_copy(samples_ref, picks_ref, sems.at[CHUNKS]),
        pltpu.make_async_copy(signs_ref, flips_ref, sems.at[CHUNKS + 1]),
    ]
    copies = []
    for chunk in range(CHUNKS):
        span = pl.ds(chunk * part, part)
        copies.append(pltpu.make_async_copy(panel_ref.at[span], rows_ref.at[span], sems.at[chunk]))
    for chunk, copy in enumerate(copies):
        copy.start(priority=chunk % 2)
    for copy in small:
        copy.start()
    small[0].wait()
    codes = coded(picks_ref[...], rows, me)
    codes_ref[...] = codes
    table = sign_rows(codes, 0, blocks, 1 - core)
    for copy in small[1:] + copies:
        copy.wait()
    for block in range(blocks):
        span = pl.ds(block * LANES, LANES)
        flipped = rows_ref[span, :] * columns_of(flips_ref[block : block + 1, :].astype(jnp.float32))
        high = flipped.astype(jnp.bfloat16)
        split_ref[span, :LANES] = high
        split_ref[span, LANES:] = (flipped - high.astype(jnp.float32)).astype(jnp.bfloat16)
    sum_samples(codes, 1 - core, split_ref, out_ref, table)


def second_kernel(codes_ref, split_ref, out_ref):
    core = lax.axis_index("dev") & 1
    sum_samples(codes_ref[...], core, split_ref, out_ref)


def local(signs, panel, samples):
    rows, width = panel.shape
    n_dev = lax.axis_size("dev")
    n_grp = lax.axis_size("grp")
    n_chip = n_dev // 2
    scale = 1.0 / math.sqrt(rows * n_dev * n_grp)
    samples = samples.reshape(-1, LANES)
    signs = signs.reshape(-1, LANES)
    vmem = pl.BlockSpec(memory_space=pltpu.VMEM)
    hbm = pl.BlockSpec(memory_space=pltpu.HBM)
    partial = pltpu.VMEM((n_chip, n_grp, SUB, LANES), jnp.float32)
    params = pltpu.CompilerParams(vmem_limit_bytes=16 << 20)
    cost = pl.CostEstimate(flops=2 * 2048 * 2048 * 256, bytes_accessed=3 << 20, transcendentals=0)

    theirs, split, codes = pl.pallas_call(
        first_kernel,
        out_shape=(partial, pltpu.VMEM((rows, 2 * LANES), jnp.bfloat16), pltpu.VMEM(samples.shape, jnp.int32)),
        in_specs=[hbm, hbm, hbm],
        out_specs=(vmem, vmem, vmem),
        scratch_shapes=[
            pltpu.VMEM(samples.shape, jnp.int32),
            pltpu.VMEM(signs.shape, jnp.int32),
            pltpu.VMEM((rows, LANES), jnp.float32),
            pltpu.SemaphoreType.DMA((CHUNKS + 2,)),
        ],
        compiler_params=params,
        cost_estimate=cost,
    )(*(pltpu.with_memory_space_constraint(value, pltpu.HBM) for value in (samples, signs, panel)))
    theirs = lax.ppermute(theirs, "dev", [(source, source ^ 1) for source in range(n_dev)])
    ours = pl.pallas_call(
        second_kernel,
        out_shape=partial,
        in_specs=[vmem, vmem],
        out_specs=vmem,
        compiler_params=params,
        cost_estimate=cost,
    )(codes, split)
    chip = ours + theirs
    plane = lax.all_to_all(
        chip.reshape(n_chip, n_grp * SUB, width),
        "dev",
        0,
        0,
        axis_index_groups=[[chip_at * 2 + side for chip_at in CHIPS] for side in range(2)],
        tiled=True,
    ).sum(axis=0) * scale
    column = lax.all_to_all(
        plane.reshape(n_grp, SUB, width),
        "grp",
        0,
        0,
        axis_index_groups=[GROUPS],
        tiled=True,
    )
    return column.sum(axis=0)


def solution(mesh):
    return jax.shard_map(
        local,
        mesh=mesh,
        in_specs=(P(("grp", "dev")), P(("grp", "dev"), None), P()),
        out_specs=P(("grp", "dev"), None),
        check_vma=False,
    )
```
